32 devices in a mesh: groups: 2 (over x), shot: 16 (over z, y, core).
Axes of the slice: x: 2, y: 2, z: 4, core: 2. Of those that a mesh axis runs over, the one named last changes fastest.
Arguments:
- courant_sq: float32 [128, 32, 128], P('groups'), parts along dimension 0, may hold values from 0.05 to 0.2
- wave_now: float32 [512, 32, 128], P(('groups', 'shot')), parts along dimension 0, may hold values from -6 to 6
- wave_before: float32 [512, 32, 128], P(('groups', 'shot')), parts along dimension 0, may hold values from -6 to 6
- wavelet: float32 [32, 8], P(('groups', 'shot')), parts along dimension 0, may hold values from -24 to 24
- source_cell: int32 [32], P(('groups', 'shot')), parts along dimension 0, may hold values from 0 to 65535, as said below
- receiver_cell: int32 [8192], P(('groups', 'shot')), parts along dimension 0, may hold values from 0 to 65535, as said below
- send_order: int32 [8192], P(('groups', 'shot')), parts along dimension 0, may hold values from 0 to 255, as said below
- observed: float32 [512, 128], P(('groups', 'shot')), parts along dimension 0, may hold values from -6 to 6
Outputs:
- gradient_slabs: float32 [128, 32, 128], P(('groups', 'shot')), parts along dimension 0
The draws below stay inside these ranges and needn't reach their ends.
There are 2 independent parts, one for each index of `groups`. The reference program is written for one: setup_inputs(seed, part) draws one part's arguments, and reference() takes and returns one part's arrays. A program takes and returns all parts, laid end to end along the dimension named above; each array names one. Nothing has to cross between parts.
Inputs may be any that keep to these rules, and one draw needn't show every extreme that they name: `source_cell`: a local cell index (x * 32 + y) * 128 + z of a block of 16 planes. `receiver_cell`: a local cell index (x * 32 + y) * 128 + z of a block of 16 planes. `send_order`: each aligned block of 256 entries is a permutation of 0 to 255.
All inputs are finite; a program needn't handle non-finite values.
Results may differ from the reference program's by a relative error of at most 0.00021.
Values sent between devices are 32-bit elements; how exact they have to be, the bound alone decides.
A program may use at most 64 MiB of HBM per device.

```python
import math
import jax
import jax.numpy as jnp

PX = 16
PY = 32
PZ = 128
NT = 8
Q = 16
RAD = 4
PIECES = 4
NX = 64
REC_DEV = 256
SHOTS = 4
N_SHOT = 16


def cell_draw(key, count):
    key_x, key_y, key_z = jax.random.split(key, 3)
    along_x = jax.random.randint(key_x, (count,), 0, PX)
    along_y = jax.random.randint(key_y, (count,), 0, PY)
    along_z = jax.random.randint(key_z, (count,), 0, PZ)
    chosen = (along_x * PY + along_y) * PZ + along_z
    chosen = chosen.at[0].set(0)
    chosen = chosen.at[1].set(PX * PY * PZ - 1)
    return chosen.astype(jnp.int32)


def draw_source_cell(key, part):
    return cell_draw(jax.random.fold_in(key, 11), N_SHOT)


def draw_receiver_cell(key, part):
    return cell_draw(jax.random.fold_in(key, 12), N_SHOT * REC_DEV)


def draw_send_order(key, part):
    keys_all = jax.random.split(jax.random.fold_in(key, 13), N_SHOT)
    orders = jax.vmap(lambda single: jax.random.permutation(single, REC_DEV))(keys_all)
    return orders.reshape(-1).astype(jnp.int32)


def shard_levels(stream_key, shape, cuts, low, high):
    factor_of = 1.0
    for axis_at, shards_of in cuts:
        draws = jax.random.uniform(jax.random.fold_in(jax.random.fold_in(stream_key, 6), axis_at), (shards_of,), jnp.float32, low / len(cuts), high / len(cuts))
        factor_of = factor_of * jnp.repeat(jnp.exp(draws), shape[axis_at] // shards_of).reshape((-1,) + (1,) * (len(shape) - 1 - axis_at))
    return factor_of


def gaussian(rng, extent, spread, limit, shards=(), kind=jnp.bfloat16):
    gain = shard_levels(rng, extent, shards, -0.22, 0.18) if shards else 1.0
    drawn = jax.random.normal(rng, extent, jnp.float32) * spread * gain
    return jnp.minimum(jnp.maximum(drawn, -limit), limit).astype(kind)


def setup_inputs(seed: int = 0, part: int = 0) -> dict:
    keys = jax.random.split(jax.random.key(seed), 9)
    part_keys = jax.random.split(jax.random.fold_in(keys[8], part), 9)
    return {
        "courant_sq": jnp.clip(jnp.exp(jax.random.uniform(part_keys[0], (NX, PY, PZ), jnp.float32, math.log(0.05), math.log(0.2))), 0.05, 0.2),
        "wave_now": gaussian(part_keys[1], (SHOTS * NX, PY, PZ), 1.0, 6.0, ((0, 16),), jnp.float32),
        "wave_before": gaussian(part_keys[2], (SHOTS * NX, PY, PZ), 1.0, 6.0, ((0, 16),), jnp.float32),
        "wavelet": gaussian(part_keys[3], (N_SHOT, NT), 4.0, 24.0, ((0, 16),), jnp.float32),
        "source_cell": draw_source_cell(jax.random.fold_in(jax.random.fold_in(keys[8], part), 71), part),
        "receiver_cell": draw_receiver_cell(jax.random.fold_in(jax.random.fold_in(keys[8], part), 71), part),
        "send_order": draw_send_order(jax.random.fold_in(jax.random.fold_in(keys[8], part), 71), part),
        "observed": gaussian(part_keys[7], (N_SHOT * N_SHOT, NT * Q), 1.0, 6.0, ((0, 16),), jnp.float32),
    }


stencil_center = -205.0 / 72.0
stencil_weights = (8.0 / 5.0, -1.0 / 5.0, 8.0 / 315.0, -1.0 / 560.0)


def laplace_whole(wavefield):
    size_x, size_y, size_z = wavefield.shape
    padded = jnp.pad(wavefield, ((0, 0), (RAD, RAD), (RAD, RAD)))

    def window(offset_y, offset_z):
        return padded[:, RAD + offset_y:RAD + offset_y + size_y, RAD + offset_z:RAD + offset_z + size_z]

    summed = 3.0 * stencil_center * wavefield
    for distance in range(1, 5):
        weight = stencil_weights[distance - 1]
        beside_all = jnp.roll(wavefield, -distance, 0) + jnp.roll(wavefield, distance, 0)
        beside_all = beside_all + window(distance, 0) + window(-distance, 0)
        beside_all = beside_all + window(0, distance) + window(0, -distance)
        summed = summed + weight * beside_all
    return summed


def inject(wavefield, cell_index, amounts):
    flattened = wavefield.reshape(-1)
    return flattened.at[cell_index].add(amounts).reshape(wavefield.shape)


def advance(current, previous, model, cell_index, amounts):
    updated = 2.0 * current - previous + model * laplace_whole(current)
    return inject(updated, cell_index, amounts)


def reference(courant_sq, wave_now, wave_before, wavelet, source_cell, receiver_cell, send_order, observed):
    periods = N_SHOT // PIECES
    cell_count = PX * PY * PZ
    model = jnp.tile(courant_sq, (periods, 1, 1))
    offsets = jnp.arange(N_SHOT, dtype=jnp.int32) * cell_count
    source_global = (source_cell + offsets).astype(jnp.int32)
    receiver_global = (receiver_cell.reshape(N_SHOT, REC_DEV) + offsets[:, None]).reshape(-1).astype(jnp.int32)

    fields = []
    current, previous = wave_now, wave_before
    for step_index in range(NT):
        updated = advance(current, previous, model, source_global, wavelet[:, step_index])
        fields.append(updated)
        previous, current = current, updated

    traces = jnp.stack([wavefield.reshape(-1)[receiver_global] for wavefield in fields])
    per_device = traces.reshape(NT, N_SHOT, REC_DEV).transpose(1, 0, 2)
    ordering = send_order.reshape(N_SHOT, REC_DEV)
    packed = jnp.take_along_axis(per_device, ordering[:, None, :], axis=2)
    arranged = packed.reshape(N_SHOT, NT, N_SHOT, Q).transpose(2, 0, 1, 3).reshape(N_SHOT * N_SHOT, NT * Q)
    misfit = arranged - observed
    returned = misfit.reshape(N_SHOT, N_SHOT, NT, Q).transpose(1, 2, 0, 3).reshape(N_SHOT, NT, REC_DEV)

    def place_rows(values, rows_order):
        return jnp.zeros((NT, REC_DEV), jnp.float32).at[:, rows_order].set(values)

    adjoint_rows = jax.vmap(place_rows)(returned, ordering)
    adjoint_global = adjoint_rows.transpose(1, 0, 2).reshape(NT, N_SHOT * REC_DEV)

    empty_field = jnp.zeros_like(wave_now)
    adjoint_now = inject(empty_field, receiver_global, adjoint_global[NT - 1])
    imaging_sum = adjoint_now * fields[NT - 1]
    adjoint_before = empty_field
    for adjoint_step in range(1, NT):
        updated = advance(adjoint_now, adjoint_before, model, receiver_global, adjoint_global[NT - 1 - adjoint_step])
        imaging_sum = imaging_sum + updated * fields[NT - 1 - adjoint_step]
        adjoint_before, adjoint_now = adjoint_now, updated

    gradient = jnp.sum(imaging_sum.reshape(periods, NX, PY, PZ), axis=0)
    slab_rows = gradient.reshape(PIECES, periods, NX // N_SHOT, PY, PZ).transpose(1, 0, 2, 3, 4).reshape(NX, PY, PZ)
    return slab_rows
```

```python
import functools

import jax
import jax.numpy as jnp
from jax import lax
from jax.experimental import pallas as pl
from jax.experimental.pallas import tpu as pltpu
from jax.sharding import PartitionSpec as P

NT = 8
PIECES = 4
MESH = pl.DeviceIdType.MESH
PAD = 8

stencil_center = -205.0 / 72.0
stencil_weights = (8.0 / 5.0, -1.0 / 5.0, 8.0 / 315.0, -1.0 / 560.0)
RAD = len(stencil_weights)


def kernel(
    count,
    courant_ref,
    now_ref,
    before_ref,
    wavelet_ref,
    source_ref,
    receiver_ref,
    order_ref,
    observed_ref,
    out_ref,
    waves,
    adjoints,
    model,
    source_mask,
    hits,
    scattered,
    image,
    row_table,
    col_table,
    spread,
    trace_out,
    trace_in,
    parts,
    load_sem,
    halo_send,
    halo_recv,
    trace_send,
    trace_recv,
    part_send,
    part_recv,
):
    planes, span_y, span_z = now_ref.shape
    receivers = receiver_ref.shape[1]
    per_owner = receivers // count
    periods = count // PIECES
    slab = planes // periods
    rows = planes * span_y
    group = lax.axis_index("groups")
    me = lax.axis_index("shot")
    left = lax.rem(me + count - 1, count)
    right = lax.rem(me + 1, count)
    piece = lax.rem(me, PIECES)
    period = me // PIECES
    inner = pl.ds(PAD, span_y)
    own = pl.ds(RAD, planes)

    loads = [
        pltpu.make_async_copy(now_ref, waves.at[1, own, inner], load_sem.at[0]),
        pltpu.make_async_copy(before_ref, waves.at[0, own, inner], load_sem.at[1]),
        pltpu.make_async_copy(
            courant_ref.at[pl.ds(piece * planes, planes)], model, load_sem.at[2]
        ),
    ]
    for load in loads:
        load.start()

    barrier = pltpu.get_barrier_semaphore()

    def greet(step, carry):
        pl.semaphore_signal(
            barrier, inc=1, device_id=(group, lax.rem(me + step, count)), device_id_type=MESH
        )
        return carry

    lax.fori_loop(1, count, greet, 0)

    for d in range(count):
        trace_out[d] = observed_ref[d : d + 1, :]

    pl.semaphore_wait(barrier, count - 1)

    def halo(field, slot, exchange, side, source=None):
        first = RAD if side == 0 else planes
        target = planes + RAD if side == 0 else 0
        if source is None:
            source = field.at[slot, pl.ds(first, RAD), inner]
        return pltpu.make_async_remote_copy(
            src_ref=source,
            dst_ref=field.at[slot, pl.ds(target, RAD), inner],
            send_sem=halo_send.at[side, exchange],
            recv_sem=halo_recv.at[side, exchange],
            device_id=(group, left if side == 0 else right),
            device_id_type=MESH,
        )

    first_sends = [
        halo(waves, 1, 0, 0, now_ref.at[pl.ds(0, RAD)]),
        halo(waves, 1, 0, 1, now_ref.at[pl.ds(planes - RAD, RAD)]),
    ]
    for send in first_sends:
        send.start()

    def trace_copy(step):
        peer = lax.rem(me + step, count)
        return pltpu.make_async_remote_copy(
            src_ref=trace_out.at[peer],
            dst_ref=trace_in.at[me],
            send_sem=trace_send.at[step],
            recv_sem=trace_recv.at[step],
            device_id=(group, peer),
            device_id_type=MESH,
        )

    def trace_start(step, carry):
        trace_copy(step).start()
        return carry

    lax.fori_loop(1, count, trace_start, 0)
    own_trace = pltpu.make_async_copy(trace_out.at[me], trace_in.at[me], load_sem.at[3])
    own_trace.start()

    edge = jnp.zeros((planes, PAD, span_z), jnp.float32)

    def clear(slot, carry):
        waves[slot, own, pl.ds(0, PAD), :] = edge
        waves[slot, own, pl.ds(PAD + span_y, PAD), :] = edge
        adjoints[slot, own, pl.ds(0, PAD), :] = edge
        adjoints[slot, own, pl.ds(PAD + span_y, PAD), :] = edge
        return carry

    lax.fori_loop(0, NT + 1, clear, 0)
    adjoints[0, own, inner, :] = jnp.zeros((planes, span_y, span_z), jnp.float32)

    cell = source_ref[0]
    flat = lax.broadcasted_iota(jnp.int32, (rows, span_z), 0) * span_z + lax.broadcasted_iota(
        jnp.int32, (rows, span_z), 1
    )
    source_mask[...] = jnp.where(flat == cell, 1.0, 0.0)

    cells = receiver_ref[...]
    order = order_ref[...]
    down = lax.broadcasted_iota(jnp.int32, (receivers, receivers), 0)
    across = lax.broadcasted_iota(jnp.int32, (receivers, receivers), 1)
    same = down == across
    cells_col = jnp.sum(jnp.where(same, cells, 0), axis=1, keepdims=True)
    order_col = jnp.sum(jnp.where(same, order, 0), axis=1, keepdims=True)
    owned_row = jnp.sum(jnp.where(down == order, cells_col, 0), axis=0, keepdims=True)
    owned_col = jnp.sum(jnp.where(across == order_col, cells, 0), axis=1, keepdims=True)
    row_table[...] = jnp.where(
        owned_row // span_z == lax.broadcasted_iota(jnp.int32, (rows, receivers), 0), 1.0, 0.0
    ).astype(jnp.bfloat16)
    col_hot = jnp.where(
        lax.rem(owned_col, span_z) == lax.broadcasted_iota(jnp.int32, (receivers, span_z), 1),
        1.0,
        0.0,
    )
    col_table[...] = col_hot
    hits[...] = jnp.dot(
        row_table[...], col_hot.astype(jnp.bfloat16), preferred_element_type=jnp.float32
    )

    lane = lax.broadcasted_iota(jnp.int32, (1, span_z), 1)
    lane_weights = []
    for distance in range(1, RAD + 1):
        weight = stencil_weights[distance - 1]
        lane_weights.append(
            (
                jnp.where(lane >= distance, weight, 0.0),
                jnp.where(lane < span_z - distance, weight, 0.0),
            )
        )

    def advanced(field, now, plane):
        at = plane + RAD
        center = field[now, at, inner, :]
        total = (3.0 * stencil_center) * center
        for distance in range(1, RAD + 1):
            beside = field[now, at + distance, inner, :] + field[now, at - distance, inner, :]
            beside = beside + (
                field[now, at, pl.ds(PAD + distance, span_y), :]
                + field[now, at, pl.ds(PAD - distance, span_y), :]
            )
            up, low = lane_weights[distance - 1]
            total = total + stencil_weights[distance - 1] * beside
            total = total + (
                up * pltpu.roll(center, distance, 1)
                + low * pltpu.roll(center, span_z - distance, 1)
            )
        return 2.0 * center - field[now - 1, at, inner, :] + model[plane] * total

    def plane_rows(plane):
        return pl.ds(pl.multiple_of(plane * span_y, span_y), span_y)

    def forward_planes(step, start):
        amount = wavelet_ref[0, step]
        made = [
            advanced(waves, step + 1, start + i)
            + amount * source_mask[plane_rows(start + i), :]
            for i in range(RAD)
        ]
        for i in range(RAD):
            waves[step + 2, start + i + RAD, inner, :] = made[i]
        return made

    def sources(step, plane, wave):
        return hits[plane_rows(plane), :] * wave - scattered[step, plane_rows(plane), :]

    def adjoint_planes(step, start, size=RAD):
        made = []
        for i in range(size):
            plane = start + i
            wave = waves[NT + 1 - step, plane + RAD, inner, :]
            made.append(advanced(adjoints, step, plane) + sources(NT - 1 - step, plane, wave))
        return made

    last = planes - RAD
    middle = range(RAD, last, RAD)

    for load in loads:
        load.wait()

    def spread_traces():
        own_trace.wait()

        def arrived(step, carry):
            trace_copy(step).wait_recv()
            return carry

        lax.fori_loop(1, count, arrived, 0)
        repeated = jnp.broadcast_to(trace_in[...], (count, per_owner, span_z)).reshape(
            receivers, span_z
        )
        slot_of = lax.rem(lax.broadcasted_iota(jnp.int32, (receivers, span_z), 0), per_owner)
        lane_slot = lax.rem(lax.broadcasted_iota(jnp.int32, (receivers, span_z), 1), per_owner)
        spread[...] = jnp.where(slot_of == lane_slot, repeated, 0.0)

    lane_step = lax.broadcasted_iota(jnp.int32, (span_z, span_z), 0) // per_owner

    def scatter(step):
        chosen = jnp.where(lane_step == step, 1.0, 0.0)
        values = jnp.dot(
            spread[...],
            chosen,
            precision=lax.Precision.HIGHEST,
            preferred_element_type=jnp.float32,
        )
        weighted = col_table[...] * values
        total = None
        for _ in range(3):
            piece_of = weighted.astype(jnp.bfloat16)
            weighted = weighted - piece_of.astype(jnp.float32)
            term = jnp.dot(row_table[...], piece_of, preferred_element_type=jnp.float32)
            total = term if total is None else total + term
        scattered[step] = total

    spread_traces()

    def forward_step(step, carry):
        halo(waves, step + 1, step, 1).wait_recv()
        forward_planes(step, 0)
        halo(waves, step + 2, step + 1, 0).start()
        halo(waves, step + 1, step, 0).wait_recv()
        forward_planes(step, last)
        halo(waves, step + 2, step + 1, 1).start()
        for start in middle:
            forward_planes(step, start)
        scatter(step)
        return carry

    lax.fori_loop(0, NT - 1, forward_step, 0)
    scatter(NT - 1)

    def begin_adjoint(start):
        made = forward_planes(NT - 1, start)
        for i in range(RAD):
            adjoints[1, start + i + RAD, inner, :] = sources(NT - 1, start + i, made[i])

    halo(waves, NT, NT - 1, 1).wait_recv()
    begin_adjoint(0)
    halo(adjoints, 1, NT, 0).start()
    halo(waves, NT, NT - 1, 0).wait_recv()
    begin_adjoint(last)
    halo(adjoints, 1, NT, 1).start()
    for start in middle:
        begin_adjoint(start)
    for plane in range(planes):
        image[plane] = (
            adjoints[1, plane + RAD, inner, :] * waves[NT + 1, plane + RAD, inner, :]
        )

    def adjoint_step(step, carry):
        def keep(start):
            made = adjoint_planes(step, start)
            for i in range(RAD):
                adjoints[step + 1, start + i + RAD, inner, :] = made[i]

        halo(adjoints, step, NT - 1 + step, 1).wait_recv()
        keep(0)
        halo(adjoints, step + 1, NT + step, 0).start()
        halo(adjoints, step, NT - 1 + step, 0).wait_recv()
        keep(last)
        halo(adjoints, step + 1, NT + step, 1).start()
        for start in middle:
            keep(start)
        for plane in range(planes):
            image[plane] += (
                adjoints[step + 1, plane + RAD, inner, :]
                * waves[NT + 1 - step, plane + RAD, inner, :]
            )
        return carry

    lax.fori_loop(1, NT - 1, adjoint_step, 0)

    halo(adjoints, NT - 1, 2 * NT - 2, 1).wait_recv()
    halo(adjoints, NT - 1, 2 * NT - 2, 0).wait_recv()

    def part_copy(step):
        target = lax.rem(period + step, periods)
        return pltpu.make_async_remote_copy(
            src_ref=image.at[pl.ds(target * slab, slab)],
            dst_ref=parts.at[step],
            send_sem=part_send.at[step],
            recv_sem=part_recv.at[step],
            device_id=(group, target * PIECES + piece),
            device_id_type=MESH,
        )

    def finish(start):
        made = adjoint_planes(NT - 1, start, slab)
        return [
            image[start + i] + made[i] * waves[2, start + i + RAD, inner, :] for i in range(slab)
        ]

    def send_part(step, carry):
        start = lax.rem(period + step, periods) * slab
        made = finish(start)
        for i in range(slab):
            image[start + i] = made[i]
        part_copy(step).start()
        return carry

    lax.fori_loop(1, periods, send_part, 0)
    start = period * slab
    made = finish(start)

    for send in first_sends:
        send.wait_send()

    def sent_wave(step, carry):
        for side in range(2):
            halo(waves, step + 1, step, side).wait_send()
        return carry

    lax.fori_loop(1, NT, sent_wave, 0)

    def sent_adjoint(step, carry):
        for side in range(2):
            halo(adjoints, step, NT - 1 + step, side).wait_send()
        return carry

    lax.fori_loop(1, NT, sent_adjoint, 0)

    def sent_trace(step, carry):
        trace_copy(step).wait_send()
        return carry

    lax.fori_loop(1, count, sent_trace, 0)

    for i in range(slab):
        out_ref[i] = made[i]

    def add_part(step, carry):
        part_copy(step).wait_recv()
        out_ref[...] += parts[step]
        return carry

    lax.fori_loop(1, periods, add_part, 0)

    def sent_part(step, carry):
        part_copy(step).wait_send()
        return carry

    lax.fori_loop(1, periods, sent_part, 0)


def per_device(
    courant_sq, wave_now, wave_before, wavelet, source_cell, receiver_cell, send_order, observed
):
    count = lax.axis_size("shot")
    planes, span_y, span_z = wave_now.shape
    receivers = receiver_cell.shape[0]
    periods = count // PIECES
    slab = planes // periods
    rows = planes * span_y
    tall = (planes + 2 * RAD, span_y + 2 * PAD, span_z)
    anywhere = pl.BlockSpec(memory_space=pl.ANY)
    scalars = pl.BlockSpec(memory_space=pltpu.SMEM)
    vectors = pl.BlockSpec(memory_space=pltpu.VMEM)
    dma = pltpu.SemaphoreType.DMA
    return pl.pallas_call(
        functools.partial(kernel, count),
        out_shape=jax.ShapeDtypeStruct((slab, span_y, span_z), jnp.float32),
        in_specs=[
            anywhere,
            anywhere,
            anywhere,
            scalars,
            scalars,
            vectors,
            vectors,
            vectors,
        ],
        out_specs=vectors,
        scratch_shapes=[
            pltpu.VMEM((NT + 2,) + tall, jnp.float32),
            pltpu.VMEM((NT + 1,) + tall, jnp.float32),
            pltpu.VMEM((planes, span_y, span_z), jnp.float32),
            pltpu.VMEM((rows, span_z), jnp.float32),
            pltpu.VMEM((rows, span_z), jnp.float32),
            pltpu.VMEM((NT, rows, span_z), jnp.float32),
            pltpu.VMEM((planes, span_y, span_z), jnp.float32),
            pltpu.VMEM((rows, receivers), jnp.bfloat16),
            pltpu.VMEM((receivers, span_z), jnp.float32),
            pltpu.VMEM((receivers, span_z), jnp.float32),
            pltpu.VMEM((count, 1, span_z), jnp.float32),
            pltpu.VMEM((count, 1, span_z), jnp.float32),
            pltpu.VMEM((periods, slab, span_y, span_z), jnp.float32),
            dma((4,)),
            dma((2, 2 * NT - 1)),
            dma((2, 2 * NT - 1)),
            dma((count,)),
            dma((count,)),
            dma((periods,)),
            dma((periods,)),
        ],
        compiler_params=pltpu.CompilerParams(
            collective_id=0, has_side_effects=True, vmem_limit_bytes=40 * 1024 * 1024
        ),
    )(
        courant_sq,
        wave_now,
        wave_before,
        wavelet,
        source_cell,
        receiver_cell.reshape(1, receivers),
        send_order.reshape(1, receivers),
        observed,
    )


def solution(mesh):
    return jax.shard_map(
        per_device,
        mesh=mesh,
        in_specs=(
            P("groups", None, None),
            P(("groups", "shot"), None, None),
            P(("groups", "shot"), None, None),
            P(("groups", "shot"), None),
            P(("groups", "shot")),
            P(("groups", "shot")),
            P(("groups", "shot")),
            P(("groups", "shot"), None),
        ),
        out_specs=P(("groups", "shot"), None, None),
        check_vma=False,
    )
```

```python
import functools

import jax
import jax.numpy as jnp
from jax import lax
from jax.experimental import pallas as pl
from jax.experimental.pallas import tpu as pltpu
from jax.sharding import PartitionSpec as P

NT = 8
PIECES = 4
MESH = pl.DeviceIdType.MESH
PAD = 8

stencil_center = -205.0 / 72.0
stencil_weights = (8.0 / 5.0, -1.0 / 5.0, 8.0 / 315.0, -1.0 / 560.0)
RAD = len(stencil_weights)
DEEP = 2 * RAD


def kernel(
    count,
    courant_ref,
    now_ref,
    before_ref,
    wavelet_ref,
    source_ref,
    receiver_ref,
    order_ref,
    observed_ref,
    out_ref,
    waves,
    adjoints,
    model,
    source_mask,
    source_note,
    hits,
    scattered,
    edge_out,
    edge_in,
    image,
    row_table,
    col_table,
    spread,
    observed,
    trace_out,
    trace_in,
    parts,
    load_sem,
    halo_send,
    halo_recv,
    first_send,
    first_recv,
    edge_send,
    edge_recv,
    trace_send,
    trace_recv,
    part_send,
    part_recv,
):
    planes, span_y, span_z = now_ref.shape
    receivers = receiver_ref.shape[1]
    per_owner = receivers // count
    periods = count // PIECES
    slab = planes // periods
    rows = planes * span_y
    model_planes = courant_ref.shape[0]
    group = lax.axis_index("groups")
    me = lax.axis_index("shot")
    left = lax.rem(me + count - 1, count)
    right = lax.rem(me + 1, count)
    piece = lax.rem(me, PIECES)
    period = me // PIECES
    inner = pl.ds(PAD, span_y)
    own = pl.ds(DEEP, planes)
    half = planes // 2

    barrier = pltpu.get_barrier_semaphore()

    def greet(step, carry):
        pl.semaphore_signal(
            barrier, inc=1, device_id=(group, lax.rem(me + step, count)), device_id_type=MESH
        )
        return carry

    lax.fori_loop(1, count, greet, 0)

    trace_load = pltpu.make_async_copy(observed_ref, observed, load_sem.at[6])
    trace_load.start()
    start_plane = piece * planes
    loads = [
        pltpu.make_async_copy(now_ref, waves.at[1, own, inner], load_sem.at[0]),
        pltpu.make_async_copy(before_ref, waves.at[0, own, inner], load_sem.at[1]),
        pltpu.make_async_copy(
            courant_ref.at[pl.ds(start_plane, planes)], model.at[pl.ds(RAD, planes)], load_sem.at[2]
        ),
        pltpu.make_async_copy(
            courant_ref.at[pl.ds(lax.rem(start_plane + model_planes - RAD, model_planes), RAD)],
            model.at[pl.ds(0, RAD)],
            load_sem.at[3],
        ),
        pltpu.make_async_copy(
            courant_ref.at[pl.ds(lax.rem(start_plane + planes, model_planes), RAD)],
            model.at[pl.ds(RAD + planes, RAD)],
            load_sem.at[4],
        ),
    ]
    for load in loads:
        load.start()

    for step in range(NT):
        source_note[1, step : step + 1, :] = jnp.full((1, span_z), wavelet_ref[0, step], jnp.float32)
    cell_value = source_ref[0].astype(jnp.float32)
    source_note[1, NT : 2 * NT, :] = jnp.full((NT, span_z), cell_value, jnp.float32)

    trace_load.wait()
    for d in range(count):
        trace_out[d] = observed[d : d + 1, :]

    def neighbour(side):
        return (group, lax.rem(me + count - 1 + 2 * side, count))

    def remote(source, target, send, recv, side):
        return pltpu.make_async_remote_copy(
            src_ref=source,
            dst_ref=target,
            send_sem=send,
            recv_sem=recv,
            device_id=neighbour(side),
            device_id_type=MESH,
        )

    def halo(field, slot, exchange, side, source=None):
        if source is None:
            source = field.at[slot, pl.ds(DEEP + half * side, DEEP), inner]
        return remote(
            source,
            field.at[slot, pl.ds((DEEP + planes) * (1 - side), DEEP), inner],
            halo_send.at[side, exchange],
            halo_recv.at[side, exchange],
            side,
        )

    def last_halo(side):
        return remote(
            adjoints.at[NT - 1, pl.ds(DEEP + (planes - RAD) * side, RAD), inner],
            adjoints.at[NT - 1, pl.ds(DEEP + planes - (planes + RAD) * side, RAD), inner],
            halo_send.at[side, NT - 1],
            halo_recv.at[side, NT - 1],
            side,
        )

    def first_halo(side):
        return halo(waves, 1, 0, side, now_ref.at[pl.ds(half * side, DEEP)])

    def before_halo(side):
        return remote(
            before_ref.at[pl.ds((planes - RAD) * side, RAD)],
            waves.at[0, pl.ds(DEEP + planes - (planes + RAD) * side, RAD), inner],
            first_send.at[side, 0],
            first_recv.at[side, 0],
            side,
        )

    def note_copy(side):
        return remote(
            source_note.at[1],
            source_note.at[2 - 2 * side],
            first_send.at[side, 1],
            first_recv.at[side, 1],
            side,
        )

    def edge_copy(which, side):
        return remote(
            edge_out.at[which, side],
            edge_in.at[which, 1 - side],
            edge_send.at[side, which],
            edge_recv.at[side, which],
            side,
        )

    def trace_copy(step):
        peer = lax.rem(me + step, count)
        return pltpu.make_async_remote_copy(
            src_ref=trace_out.at[peer],
            dst_ref=trace_in.at[me],
            send_sem=trace_send.at[step],
            recv_sem=trace_recv.at[step],
            device_id=(group, peer),
            device_id_type=MESH,
        )

    pl.semaphore_wait(barrier, count - 1)
    for side in range(2):
        first_halo(side).start()
    for side in range(2):
        before_halo(side).start()
        note_copy(side).start()

    def trace_start(step, carry):
        trace_copy(step).start()
        return carry

    lax.fori_loop(1, count, trace_start, 0)
    own_trace = pltpu.make_async_copy(trace_out.at[me], trace_in.at[me], load_sem.at[5])
    own_trace.start()

    wide = pl.ds(DEEP - RAD, planes + 2 * RAD)
    blank = jnp.zeros((planes + 2 * RAD, PAD, span_z), jnp.float32)

    def clear(slot, carry):
        waves[slot, wide, pl.ds(0, PAD), :] = blank
        waves[slot, wide, pl.ds(PAD + span_y, PAD), :] = blank
        adjoints[slot, wide, pl.ds(0, PAD), :] = blank
        adjoints[slot, wide, pl.ds(PAD + span_y, PAD), :] = blank
        return carry

    lax.fori_loop(0, NT, clear, 0)
    waves[NT, wide, pl.ds(0, PAD), :] = blank
    waves[NT, wide, pl.ds(PAD + span_y, PAD), :] = blank
    adjoints[0, wide, inner, :] = jnp.zeros((planes + 2 * RAD, span_y, span_z), jnp.float32)

    def cells_from(plane, size):
        shape = (size * span_y, span_z)
        flat = lax.broadcasted_iota(jnp.int32, shape, 0) * span_z
        flat = flat + lax.broadcasted_iota(jnp.int32, shape, 1) + plane * (span_y * span_z)
        return flat.astype(jnp.float32)

    def mark_source(place, size, plane, owner):
        marked = jnp.where(
            cells_from(plane, size) == source_note[owner, NT : NT + 1, :], 1.0, 0.0
        )
        source_mask[pl.ds(place, size)] = marked.reshape(size, span_y, span_z)

    mark_source(RAD, planes, 0, 1)

    cells = receiver_ref[...]
    order = order_ref[...]
    down = lax.broadcasted_iota(jnp.int32, (receivers, receivers), 0)
    across = lax.broadcasted_iota(jnp.int32, (receivers, receivers), 1)
    same = down == across
    cells_col = jnp.sum(jnp.where(same, cells, 0), axis=1, keepdims=True)
    order_col = jnp.sum(jnp.where(same, order, 0), axis=1, keepdims=True)
    owned_row = jnp.sum(jnp.where(down == order, cells_col, 0), axis=0, keepdims=True)
    owned_col = jnp.sum(jnp.where(across == order_col, cells, 0), axis=1, keepdims=True)
    row_table[...] = jnp.where(
        owned_row // span_z == lax.broadcasted_iota(jnp.int32, (rows, receivers), 0), 1.0, 0.0
    ).astype(jnp.bfloat16)
    col_hot = jnp.where(
        lax.rem(owned_col, span_z) == lax.broadcasted_iota(jnp.int32, (receivers, span_z), 1),
        1.0,
        0.0,
    )
    col_table[...] = col_hot
    hits[...] = jnp.dot(
        row_table[...], col_hot.astype(jnp.bfloat16), preferred_element_type=jnp.float32
    )

    lane = lax.broadcasted_iota(jnp.int32, (1, span_z), 1)
    lane_weights = []
    for distance in range(1, RAD + 1):
        weight = stencil_weights[distance - 1]
        lane_weights.append(
            (
                jnp.where(lane >= distance, weight, 0.0),
                jnp.where(lane < span_z - distance, weight, 0.0),
            )
        )

    def advanced(field, now, plane):
        at = plane + DEEP
        center = field[now, at, inner, :]
        total = (3.0 * stencil_center) * center
        for distance in range(1, RAD + 1):
            beside = field[now, at + distance, inner, :] + field[now, at - distance, inner, :]
            beside = beside + (
                field[now, at, pl.ds(PAD + distance, span_y), :]
                + field[now, at, pl.ds(PAD - distance, span_y), :]
            )
            up, low = lane_weights[distance - 1]
            total = total + stencil_weights[distance - 1] * beside
            total = total + (
                up * pltpu.roll(center, distance, 1)
                + low * pltpu.roll(center, span_z - distance, 1)
            )
        return 2.0 * center - field[now - 1, at, inner, :] + model[plane + RAD] * total

    def plane_rows(plane):
        return pl.ds(pl.multiple_of(plane * span_y, span_y), span_y)

    def store(field, slot, start, made):
        for i in range(len(made)):
            field[slot, start + i + DEEP, inner, :] = made[i]

    def forward_planes(step, start, owner=1):
        amount = source_note[owner, pl.ds(step, 1), :]
        made = [
            advanced(waves, step + 1, start + i) + amount * source_mask[start + i + RAD]
            for i in range(RAD)
        ]
        store(waves, step + 2, start, made)
        return made

    def sources(step, plane, wave):
        return hits[plane_rows(plane), :] * wave - scattered[step, plane_rows(plane), :]

    def adjoint_planes(step, start, size=RAD):
        made = []
        for i in range(size):
            plane = start + i
            wave = waves[NT + 1 - step, plane + DEEP, inner, :]
            made.append(advanced(adjoints, step, plane) + sources(NT - 1 - step, plane, wave))
        return made

    def adjoint_keep(step, start):
        store(adjoints, step + 1, start, adjoint_planes(step, start))

    def adjoint_beside(step, start, which, side):
        made = [
            advanced(adjoints, step, start + i) + edge_in[which, side, i] for i in range(RAD)
        ]
        store(adjoints, step + 1, start, made)

    def send_edges(which, step, side):
        start = (planes - RAD) * side
        for i in range(RAD):
            wave = waves[step + 2, start + i + DEEP, inner, :]
            edge_out[which, side, i] = sources(step, start + i, wave)
        edge_copy(which, side).start()

    middle = range(RAD, planes - RAD, RAD)

    def spread_traces():
        own_trace.wait()

        def arrived(step, carry):
            trace_copy(step).wait_recv()
            return carry

        lax.fori_loop(1, count, arrived, 0)
        repeated = jnp.broadcast_to(trace_in[...], (count, per_owner, span_z)).reshape(
            receivers, span_z
        )
        slot_of = lax.rem(lax.broadcasted_iota(jnp.int32, (receivers, span_z), 0), per_owner)
        lane_slot = lax.rem(lax.broadcasted_iota(jnp.int32, (receivers, span_z), 1), per_owner)
        spread[...] = jnp.where(slot_of == lane_slot, repeated, 0.0)

    lane_step = lax.broadcasted_iota(jnp.int32, (span_z, span_z), 0) // per_owner

    def scatter(step):
        chosen = jnp.where(lane_step == step, 1.0, 0.0)
        values = jnp.dot(
            spread[...],
            chosen,
            precision=lax.Precision.HIGHEST,
            preferred_element_type=jnp.float32,
        )
        weighted = col_table[...] * values
        total = None
        for _ in range(3):
            piece_of = weighted.astype(jnp.bfloat16)
            weighted = weighted - piece_of.astype(jnp.float32)
            term = jnp.dot(row_table[...], piece_of, preferred_element_type=jnp.float32)
            total = term if total is None else total + term
        scattered[step] = total

    for load in loads:
        load.wait()

    first_side = lax.rem(me, 2)

    def forward_pair(pair, begin_adjoint):
        step = 2 * pair
        for start in middle:
            forward_planes(step, start)

        def one_side(turn, carry):
            side = lax.rem(first_side + turn, 2)
            halo(waves, step + 1, pair, 1 - side).wait_recv()

            if not begin_adjoint:

                @pl.when(pair == 0)
                def _():
                    before_halo(1 - side).wait_recv()
                    note_copy(1 - side).wait_recv()
                    mark_source(
                        (planes + RAD) * side, RAD, (planes - RAD) * (1 - side), 2 * side
                    )

            forward_planes(step, (planes + RAD) * side - RAD, 2 * side)
            forward_planes(step, (planes - RAD) * side)
            for part in range(0, half, RAD):
                start = half * side + part
                made = forward_planes(step + 1, start)
                if begin_adjoint:
                    first = [
                        sources(NT - 1, start + i, made[i]) for i in range(RAD)
                    ]
                    store(adjoints, 1, start, first)
            if begin_adjoint:
                halo(adjoints, 1, NT // 2, side).start()
                send_edges(NT // 2 - 2, NT - 2, side)
            else:
                halo(waves, step + 3, pair + 1, side).start()
            return carry

        lax.fori_loop(0, 2, one_side, 0)

    def forward_loop(pair, carry):
        forward_pair(pair, False)

        @pl.when(pair == 0)
        def _():
            spread_traces()

        for i in range(3):
            scatter(3 * pair + i)

        @pl.when(pair > 0)
        def _():
            for side in range(2):
                send_edges(pair - 1, 2 * pair, side)

        return carry

    lax.fori_loop(0, NT // 2 - 1, forward_loop, 0)
    forward_pair(NT // 2 - 1, True)

    def add_image(step):
        for plane in range(planes):
            image[plane] += (
                adjoints[step, plane + DEEP, inner, :]
                * waves[NT + 2 - step, plane + DEEP, inner, :]
            )

    image[...] = jnp.zeros((planes, span_y, span_z), jnp.float32)

    def adjoint_pair(pair, last):
        step = 2 * pair + 1
        which = NT // 2 - 2 - pair
        for start in middle:
            adjoint_keep(step, start)

        def one_side(turn, carry):
            side = lax.rem(first_side + turn, 2)
            halo(adjoints, step, NT // 2 + pair, 1 - side).wait_recv()
            edge_copy(which, 1 - side).wait_recv()
            adjoint_beside(step, (planes + RAD) * side - RAD, which, side)
            adjoint_keep(step, (planes - RAD) * side)
            if last:
                adjoint_keep(step + 1, (planes - RAD) * side)
                last_halo(side).start()
            else:
                for part in range(0, half, RAD):
                    adjoint_keep(step + 1, half * side + part)
                halo(adjoints, step + 2, NT // 2 + pair + 1, side).start()
            return carry

        lax.fori_loop(0, 2, one_side, 0)
        if last:
            for start in middle:
                adjoint_keep(step + 1, start)
        add_image(step)
        add_image(step + 1)

    def adjoint_loop(pair, carry):
        adjoint_pair(pair, False)
        return carry

    lax.fori_loop(0, NT // 2 - 2, adjoint_loop, 0)
    adjoint_pair(NT // 2 - 2, True)
    add_image(NT - 1)

    for side in range(2):
        last_halo(side).wait_recv()

    def part_copy(step):
        target = lax.rem(period + step, periods)
        return pltpu.make_async_remote_copy(
            src_ref=image.at[pl.ds(target * slab, slab)],
            dst_ref=parts.at[step],
            send_sem=part_send.at[step],
            recv_sem=part_recv.at[step],
            device_id=(group, target * PIECES + piece),
            device_id_type=MESH,
        )

    def finish(start):
        made = adjoint_planes(NT - 1, start, slab)
        return [
            image[start + i] + made[i] * waves[2, start + i + DEEP, inner, :] for i in range(slab)
        ]

    def send_part(step, carry):
        start = lax.rem(period + step, periods) * slab
        made = finish(start)
        for i in range(slab):
            image[start + i] = made[i]
        part_copy(step).start()
        return carry

    lax.fori_loop(1, periods, send_part, 0)
    start = period * slab
    made = finish(start)
    for i in range(slab):
        out_ref[i] = made[i]

    for side in range(2):
        first_halo(side).wait_send()
        before_halo(side).wait_send()
        note_copy(side).wait_send()
        last_halo(side).wait_send()
        for pair in range(1, NT // 2):
            halo(waves, 2 * pair + 1, pair, side).wait_send()
            halo(adjoints, 2 * pair - 1, NT // 2 + pair - 1, side).wait_send()
            edge_copy(pair - 1, side).wait_send()

    def sent_trace(step, carry):
        trace_copy(step).wait_send()
        return carry

    lax.fori_loop(1, count, sent_trace, 0)

    def add_part(step, carry):
        part_copy(step).wait_recv()
        out_ref[...] += parts[step]
        return carry

    lax.fori_loop(1, periods, add_part, 0)

    def sent_part(step, carry):
        part_copy(step).wait_send()
        return carry

    lax.fori_loop(1, periods, sent_part, 0)


def per_device(
    courant_sq, wave_now, wave_before, wavelet, source_cell, receiver_cell, send_order, observed
):
    count = lax.axis_size("shot")
    planes, span_y, span_z = wave_now.shape
    receivers = receiver_cell.shape[0]
    periods = count // PIECES
    slab = planes // periods
    rows = planes * span_y
    tall = (planes + 2 * DEEP, span_y + 2 * PAD, span_z)
    anywhere = pl.BlockSpec(memory_space=pltpu.HBM)
    scalars = pl.BlockSpec(memory_space=pltpu.SMEM)
    vectors = pl.BlockSpec(memory_space=pltpu.VMEM)
    dma = pltpu.SemaphoreType.DMA
    return pl.pallas_call(
        functools.partial(kernel, count),
        out_shape=jax.ShapeDtypeStruct((slab, span_y, span_z), jnp.float32),
        in_specs=[
            anywhere,
            anywhere,
            anywhere,
            scalars,
            scalars,
            vectors,
            vectors,
            anywhere,
        ],
        out_specs=vectors,
        scratch_shapes=[
            pltpu.VMEM((NT + 2,) + tall, jnp.float32),
            pltpu.VMEM((NT,) + tall, jnp.float32),
            pltpu.VMEM((planes + 2 * RAD, span_y, span_z), jnp.float32),
            pltpu.VMEM((planes + 2 * RAD, span_y, span_z), jnp.float32),
            pltpu.VMEM((3, 2 * NT, span_z), jnp.float32),
            pltpu.VMEM((rows, span_z), jnp.float32),
            pltpu.VMEM((NT + 1, rows, span_z), jnp.float32),
            pltpu.VMEM((NT // 2 - 1, 2, RAD, span_y, span_z), jnp.float32),
            pltpu.VMEM((NT // 2 - 1, 2, RAD, span_y, span_z), jnp.float32),
            pltpu.VMEM((planes, span_y, span_z), jnp.float32),
            pltpu.VMEM((rows, receivers), jnp.bfloat16),
            pltpu.VMEM((receivers, span_z), jnp.float32),
            pltpu.VMEM((receivers, span_z), jnp.float32),
            pltpu.VMEM((count, span_z), jnp.float32),
            pltpu.VMEM((count, 1, span_z), jnp.float32),
            pltpu.VMEM((count, 1, span_z), jnp.float32),
            pltpu.VMEM((periods, slab, span_y, span_z), jnp.float32),
            dma((7,)),
            dma((2, NT)),
            dma((2, NT)),
            dma((2, 2)),
            dma((2, 2)),
            dma((2, NT // 2 - 1)),
            dma((2, NT // 2 - 1)),
            dma((count,)),
            dma((count,)),
            dma((periods,)),
            dma((periods,)),
        ],
        compiler_params=pltpu.CompilerParams(
            collective_id=0, has_side_effects=True, vmem_limit_bytes=63 * 1024 * 1024
        ),
    )(
        courant_sq,
        wave_now,
        wave_before,
        wavelet,
        source_cell,
        receiver_cell.reshape(1, receivers),
        send_order.reshape(1, receivers),
        observed,
    )


def solution(mesh):
    return jax.shard_map(
        per_device,
        mesh=mesh,
        in_specs=(
            P("groups", None, None),
            P(("groups", "shot"), None, None),
            P(("groups", "shot"), None, None),
            P(("groups", "shot"), None),
            P(("groups", "shot")),
            P(("groups", "shot")),
            P(("groups", "shot")),
            P(("groups", "shot"), None),
        ),
        out_specs=P(("groups", "shot"), None, None),
        check_vma=False,
    )
```

```python
import functools

import jax
import jax.numpy as jnp
from jax import lax
from jax.experimental import pallas as pl
from jax.experimental.pallas import tpu as pltpu
from jax.sharding import PartitionSpec as P

NT = 8
PIECES = 4
MESH = pl.DeviceIdType.MESH
PAD = 8

stencil_center = -205.0 / 72.0
stencil_weights = (8.0 / 5.0, -1.0 / 5.0, 8.0 / 315.0, -1.0 / 560.0)
RAD = len(stencil_weights)
DEEP = 2 * RAD


def kernel(
    count,
    courant_ref,
    now_ref,
    before_ref,
    wavelet_ref,
    source_ref,
    receiver_ref,
    order_ref,
    observed_ref,
    out_ref,
    waves,
    adjoints,
    model,
    source_mask,
    source_note,
    hits,
    scattered,
    edge_out,
    edge_in,
    image,
    row_table,
    col_table,
    spread,
    observed,
    trace_out,
    trace_in,
    parts,
    load_sem,
    halo_send,
    halo_recv,
    first_send,
    first_recv,
    edge_send,
    edge_recv,
    trace_send,
    trace_recv,
    part_send,
    part_recv,
):
    planes, span_y, span_z = now_ref.shape
    receivers = receiver_ref.shape[1]
    per_owner = receivers // count
    periods = count // PIECES
    slab = planes // periods
    rows = planes * span_y
    model_planes = courant_ref.shape[0]
    group = lax.axis_index("groups")
    me = lax.axis_index("shot")
    left = lax.rem(me + count - 1, count)
    right = lax.rem(me + 1, count)
    piece = lax.rem(me, PIECES)
    period = me // PIECES
    inner = pl.ds(PAD, span_y)
    own = pl.ds(DEEP, planes)
    half = planes // 2

    barrier = pltpu.get_barrier_semaphore()

    def greet(step, carry):
        pl.semaphore_signal(
            barrier, inc=1, device_id=(group, lax.rem(me + step, count)), device_id_type=MESH
        )
        return carry

    lax.fori_loop(1, count, greet, 0)

    trace_load = pltpu.make_async_copy(observed_ref, observed, load_sem.at[6])
    trace_load.start()
    start_plane = piece * planes
    loads = [
        pltpu.make_async_copy(now_ref, waves.at[1, own, inner], load_sem.at[0]),
        pltpu.make_async_copy(before_ref, waves.at[0, own, inner], load_sem.at[1]),
        pltpu.make_async_copy(
            courant_ref.at[pl.ds(start_plane, planes)], model.at[pl.ds(RAD, planes)], load_sem.at[2]
        ),
        pltpu.make_async_copy(
            courant_ref.at[pl.ds(lax.rem(start_plane + model_planes - RAD, model_planes), RAD)],
            model.at[pl.ds(0, RAD)],
            load_sem.at[3],
        ),
        pltpu.make_async_copy(
            courant_ref.at[pl.ds(lax.rem(start_plane + planes, model_planes), RAD)],
            model.at[pl.ds(RAD + planes, RAD)],
            load_sem.at[4],
        ),
    ]
    for load in loads:
        load.start()

    for step in range(NT):
        source_note[1, step : step + 1, :] = jnp.full((1, span_z), wavelet_ref[0, step], jnp.float32)
    cell_value = source_ref[0].astype(jnp.float32)
    source_note[1, NT : 2 * NT, :] = jnp.full((NT, span_z), cell_value, jnp.float32)

    trace_load.wait()
    for d in range(count):
        trace_out[d] = observed[d : d + 1, :]

    def neighbour(side):
        return (group, lax.rem(me + count - 1 + 2 * side, count))

    def remote(source, target, send, recv, side):
        return pltpu.make_async_remote_copy(
            src_ref=source,
            dst_ref=target,
            send_sem=send,
            recv_sem=recv,
            device_id=neighbour(side),
            device_id_type=MESH,
        )

    def halo(field, slot, exchange, side, source=None):
        if source is None:
            source = field.at[slot, pl.ds(DEEP + half * side, DEEP), inner]
        return remote(
            source,
            field.at[slot, pl.ds((DEEP + planes) * (1 - side), DEEP), inner],
            halo_send.at[side, exchange],
            halo_recv.at[side, exchange],
            side,
        )

    def last_halo(side):
        return remote(
            adjoints.at[NT - 1, pl.ds(DEEP + (planes - RAD) * side, RAD), inner],
            adjoints.at[NT - 1, pl.ds(DEEP + planes - (planes + RAD) * side, RAD), inner],
            halo_send.at[side, NT - 1],
            halo_recv.at[side, NT - 1],
            side,
        )

    def first_halo(side):
        return halo(waves, 1, 0, side, now_ref.at[pl.ds(half * side, DEEP)])

    def before_halo(side):
        return remote(
            before_ref.at[pl.ds((planes - RAD) * side, RAD)],
            waves.at[0, pl.ds(DEEP + planes - (planes + RAD) * side, RAD), inner],
            first_send.at[side, 0],
            first_recv.at[side, 0],
            side,
        )

    def note_copy(side):
        return remote(
            source_note.at[1],
            source_note.at[2 - 2 * side],
            first_send.at[side, 1],
            first_recv.at[side, 1],
            side,
        )

    def edge_copy(which, side):
        return remote(
            edge_out.at[which, side],
            edge_in.at[which, 1 - side],
            edge_send.at[side, which],
            edge_recv.at[side, which],
            side,
        )

    def trace_copy(step):
        peer = lax.rem(me + step, count)
        return pltpu.make_async_remote_copy(
            src_ref=trace_out.at[peer],
            dst_ref=trace_in.at[me],
            send_sem=trace_send.at[step],
            recv_sem=trace_recv.at[step],
            device_id=(group, peer),
            device_id_type=MESH,
        )

    pl.semaphore_wait(barrier, count - 1)
    for side in range(2):
        first_halo(side).start()
    for side in range(2):
        before_halo(side).start()
        note_copy(side).start()

    def trace_start(step, carry):
        trace_copy(step).start()
        return carry

    lax.fori_loop(1, count, trace_start, 0)
    own_trace = pltpu.make_async_copy(trace_out.at[me], trace_in.at[me], load_sem.at[5])
    own_trace.start()

    wide = pl.ds(DEEP - RAD, planes + 2 * RAD)
    blank = jnp.zeros((planes + 2 * RAD, PAD, span_z), jnp.float32)

    def clear(slot, carry):
        waves[slot, wide, pl.ds(0, PAD), :] = blank
        waves[slot, wide, pl.ds(PAD + span_y, PAD), :] = blank
        adjoints[slot, wide, pl.ds(0, PAD), :] = blank
        adjoints[slot, wide, pl.ds(PAD + span_y, PAD), :] = blank
        return carry

    lax.fori_loop(0, NT, clear, 0)
    waves[NT, wide, pl.ds(0, PAD), :] = blank
    waves[NT, wide, pl.ds(PAD + span_y, PAD), :] = blank
    adjoints[0, wide, inner, :] = jnp.zeros((planes + 2 * RAD, span_y, span_z), jnp.float32)

    def cells_from(plane, size):
        shape = (size * span_y, span_z)
        flat = lax.broadcasted_iota(jnp.int32, shape, 0) * span_z
        flat = flat + lax.broadcasted_iota(jnp.int32, shape, 1) + plane * (span_y * span_z)
        return flat.astype(jnp.float32)

    def mark_source(place, size, plane, owner):
        marked = jnp.where(
            cells_from(plane, size) == source_note[owner, NT : NT + 1, :], 1.0, 0.0
        )
        source_mask[pl.ds(place, size)] = marked.reshape(size, span_y, span_z)

    mark_source(RAD, planes, 0, 1)

    cells = receiver_ref[...]
    order = order_ref[...]
    down = lax.broadcasted_iota(jnp.int32, (receivers, receivers), 0)
    across = lax.broadcasted_iota(jnp.int32, (receivers, receivers), 1)
    same = down == across
    cells_col = jnp.sum(jnp.where(same, cells, 0), axis=1, keepdims=True)
    order_col = jnp.sum(jnp.where(same, order, 0), axis=1, keepdims=True)
    owned_row = jnp.sum(jnp.where(down == order, cells_col, 0), axis=0, keepdims=True)
    owned_col = jnp.sum(jnp.where(across == order_col, cells, 0), axis=1, keepdims=True)
    row_table[...] = jnp.where(
        owned_row // span_z == lax.broadcasted_iota(jnp.int32, (rows, receivers), 0), 1.0, 0.0
    ).astype(jnp.bfloat16)
    col_hot = jnp.where(
        lax.rem(owned_col, span_z) == lax.broadcasted_iota(jnp.int32, (receivers, span_z), 1),
        1.0,
        0.0,
    )
    col_table[...] = col_hot
    hits[...] = jnp.dot(
        row_table[...], col_hot.astype(jnp.bfloat16), preferred_element_type=jnp.float32
    )

    lane = lax.broadcasted_iota(jnp.int32, (1, 1, span_z), 2)
    lane_weights = []
    for distance in range(1, RAD + 1):
        weight = stencil_weights[distance - 1]
        lane_weights.append(
            (
                jnp.where(lane >= distance, weight, 0.0),
                jnp.where(lane < span_z - distance, weight, 0.0),
            )
        )

    def advanced(field, now, start, size=RAD):
        tiles = []
        for row in range(0, span_y, PAD):
            column = field[
                now, pl.ds(start + DEEP - RAD, size + 2 * RAD), pl.ds(PAD + row, PAD), :
            ]
            here = pl.ds(start + DEEP, size)
            center = column[RAD : RAD + size]
            total = (3.0 * stencil_center) * center
            for distance in range(1, RAD + 1):
                beside = (
                    column[RAD + distance : RAD + distance + size]
                    + column[RAD - distance : RAD - distance + size]
                )
                beside = beside + (
                    field[now, here, pl.ds(PAD + row + distance, PAD), :]
                    + field[now, here, pl.ds(PAD + row - distance, PAD), :]
                )
                up, low = lane_weights[distance - 1]
                total = total + stencil_weights[distance - 1] * beside
                total = total + (
                    up * pltpu.roll(center, distance, 2)
                    + low * pltpu.roll(center, span_z - distance, 2)
                )
            tiles.append(
                2.0 * center
                - field[now - 1, here, pl.ds(PAD + row, PAD), :]
                + model[pl.ds(start + RAD, size), pl.ds(row, PAD), :] * total
            )
        return jnp.concatenate(tiles, axis=1)

    def plane_rows(plane):
        return pl.ds(pl.multiple_of(plane * span_y, span_y), span_y)

    def store(field, slot, start, made):
        for i in range(len(made)):
            field[slot, start + i + DEEP, inner, :] = made[i]

    def forward_planes(step, start, owner=1):
        amount = source_note[owner, pl.ds(step, 1), :]
        ahead = advanced(waves, step + 1, start)
        made = [ahead[i] + amount * source_mask[start + i + RAD] for i in range(RAD)]
        store(waves, step + 2, start, made)
        return made

    def sources(step, plane, wave):
        return hits[plane_rows(plane), :] * wave - scattered[step, plane_rows(plane), :]

    def adjoint_planes(step, start, size=RAD):
        made = []
        ahead = advanced(adjoints, step, start, size)
        for i in range(size):
            plane = start + i
            wave = waves[NT + 1 - step, plane + DEEP, inner, :]
            made.append(ahead[i] + sources(NT - 1 - step, plane, wave))
        return made

    def adjoint_keep(step, start):
        store(adjoints, step + 1, start, adjoint_planes(step, start))

    def adjoint_beside(step, start, which, side):
        ahead = advanced(adjoints, step, start)
        made = [ahead[i] + edge_in[which, side, i] for i in range(RAD)]
        store(adjoints, step + 1, start, made)

    def send_edges(which, step, side):
        start = (planes - RAD) * side
        for i in range(RAD):
            wave = waves[step + 2, start + i + DEEP, inner, :]
            edge_out[which, side, i] = sources(step, start + i, wave)
        edge_copy(which, side).start()

    middle = range(RAD, planes - RAD, RAD)

    def spread_traces():
        own_trace.wait()

        def arrived(step, carry):
            trace_copy(step).wait_recv()
            return carry

        lax.fori_loop(1, count, arrived, 0)
        repeated = jnp.broadcast_to(trace_in[...], (count, per_owner, span_z)).reshape(
            receivers, span_z
        )
        slot_of = lax.rem(lax.broadcasted_iota(jnp.int32, (receivers, span_z), 0), per_owner)
        lane_slot = lax.rem(lax.broadcasted_iota(jnp.int32, (receivers, span_z), 1), per_owner)
        spread[...] = jnp.where(slot_of == lane_slot, repeated, 0.0)

    lane_step = lax.broadcasted_iota(jnp.int32, (span_z, span_z), 0) // per_owner

    def scatter(step):
        chosen = jnp.where(lane_step == step, 1.0, 0.0)
        values = jnp.dot(
            spread[...],
            chosen,
            precision=lax.Precision.HIGHEST,
            preferred_element_type=jnp.float32,
        )
        weighted = col_table[...] * values
        total = None
        for _ in range(3):
            piece_of = weighted.astype(jnp.bfloat16)
            weighted = weighted - piece_of.astype(jnp.float32)
            term = jnp.dot(row_table[...], piece_of, preferred_element_type=jnp.float32)
            total = term if total is None else total + term
        scattered[step] = total

    for load in loads:
        load.wait()

    first_side = lax.rem(me, 2)

    def forward_pair(pair, begin_adjoint):
        step = 2 * pair
        for start in middle:
            forward_planes(step, start)

        def one_side(turn, carry):
            side = lax.rem(first_side + turn, 2)
            halo(waves, step + 1, pair, 1 - side).wait_recv()

            if not begin_adjoint:

                @pl.when(pair == 0)
                def _():
                    before_halo(1 - side).wait_recv()
                    note_copy(1 - side).wait_recv()
                    mark_source(
                        (planes + RAD) * side, RAD, (planes - RAD) * (1 - side), 2 * side
                    )

            forward_planes(step, (planes + RAD) * side - RAD, 2 * side)
            forward_planes(step, (planes - RAD) * side)
            for part in range(0, half, RAD):
                start = half * side + part
                made = forward_planes(step + 1, start)
                if begin_adjoint:
                    first = [
                        sources(NT - 1, start + i, made[i]) for i in range(RAD)
                    ]
                    store(adjoints, 1, start, first)
            if begin_adjoint:
                halo(adjoints, 1, NT // 2, side).start()
                send_edges(NT // 2 - 2, NT - 2, side)
            else:
                halo(waves, step + 3, pair + 1, side).start()
            return carry

        lax.fori_loop(0, 2, one_side, 0)

    def forward_loop(pair, carry):
        forward_pair(pair, False)

        @pl.when(pair == 0)
        def _():
            spread_traces()

        for i in range(3):
            scatter(3 * pair + i)

        @pl.when(pair > 0)
        def _():
            for side in range(2):
                send_edges(pair - 1, 2 * pair, side)

        return carry

    lax.fori_loop(0, NT // 2 - 1, forward_loop, 0)
    forward_pair(NT // 2 - 1, True)

    def add_image(step):
        for plane in range(planes):
            image[plane] += (
                adjoints[step, plane + DEEP, inner, :]
                * waves[NT + 2 - step, plane + DEEP, inner, :]
            )

    image[...] = jnp.zeros((planes, span_y, span_z), jnp.float32)

    def adjoint_pair(pair, last):
        step = 2 * pair + 1
        which = NT // 2 - 2 - pair
        for start in middle:
            adjoint_keep(step, start)

        def one_side(turn, carry):
            side = lax.rem(first_side + turn, 2)
            halo(adjoints, step, NT // 2 + pair, 1 - side).wait_recv()
            edge_copy(which, 1 - side).wait_recv()
            adjoint_beside(step, (planes + RAD) * side - RAD, which, side)
            adjoint_keep(step, (planes - RAD) * side)
            if last:
                adjoint_keep(step + 1, (planes - RAD) * side)
                last_halo(side).start()
            else:
                for part in range(0, half, RAD):
                    adjoint_keep(step + 1, half * side + part)
                halo(adjoints, step + 2, NT // 2 + pair + 1, side).start()
            return carry

        lax.fori_loop(0, 2, one_side, 0)
        if last:
            for start in middle:
                adjoint_keep(step + 1, start)
        add_image(step)
        add_image(step + 1)

    def adjoint_loop(pair, carry):
        adjoint_pair(pair, False)
        return carry

    lax.fori_loop(0, NT // 2 - 2, adjoint_loop, 0)
    adjoint_pair(NT // 2 - 2, True)
    add_image(NT - 1)

    def part_copy(step):
        target = lax.rem(period + step, periods)
        return pltpu.make_async_remote_copy(
            src_ref=image.at[pl.ds(target * slab, slab)],
            dst_ref=parts.at[step],
            send_sem=part_send.at[step],
            recv_sem=part_recv.at[step],
            device_id=(group, target * PIECES + piece),
            device_id_type=MESH,
        )

    def finish(start):
        made = adjoint_planes(NT - 1, start, slab)
        return [
            image[start + i] + made[i] * waves[2, start + i + DEEP, inner, :] for i in range(slab)
        ]

    def send_part(which, carry):
        start = which * slab
        made = finish(start)
        for i in range(slab):
            image[start + i] = made[i]

        @pl.when(which != period)
        def _():
            part_copy(lax.rem(which - period + periods, periods)).start()

        return carry

    low, high = RAD // slab, (planes - RAD) // slab
    lax.fori_loop(low, high, send_part, 0)
    for side in range(2):
        last_halo(side).wait_recv()
    lax.fori_loop(0, low, send_part, 0)
    lax.fori_loop(high, periods, send_part, 0)
    for i in range(slab):
        out_ref[i] = image[period * slab + i]

    for side in range(2):
        first_halo(side).wait_send()
        before_halo(side).wait_send()
        note_copy(side).wait_send()
        last_halo(side).wait_send()
        for pair in range(1, NT // 2):
            halo(waves, 2 * pair + 1, pair, side).wait_send()
            halo(adjoints, 2 * pair - 1, NT // 2 + pair - 1, side).wait_send()
            edge_copy(pair - 1, side).wait_send()

    def sent_trace(step, carry):
        trace_copy(step).wait_send()
        return carry

    lax.fori_loop(1, count, sent_trace, 0)

    def add_part(step, carry):
        part_copy(step).wait_recv()
        out_ref[...] += parts[step]
        return carry

    lax.fori_loop(1, periods, add_part, 0)

    def sent_part(step, carry):
        part_copy(step).wait_send()
        return carry

    lax.fori_loop(1, periods, sent_part, 0)


def per_device(
    courant_sq, wave_now, wave_before, wavelet, source_cell, receiver_cell, send_order, observed
):
    count = lax.axis_size("shot")
    planes, span_y, span_z = wave_now.shape
    receivers = receiver_cell.shape[0]
    periods = count // PIECES
    slab = planes // periods
    rows = planes * span_y
    tall = (planes + 2 * DEEP, span_y + 2 * PAD, span_z)
    anywhere = pl.BlockSpec(memory_space=pltpu.HBM)
    scalars = pl.BlockSpec(memory_space=pltpu.SMEM)
    vectors = pl.BlockSpec(memory_space=pltpu.VMEM)
    dma = pltpu.SemaphoreType.DMA
    return pl.pallas_call(
        functools.partial(kernel, count),
        out_shape=jax.ShapeDtypeStruct((slab, span_y, span_z), jnp.float32),
        in_specs=[
            anywhere,
            anywhere,
            anywhere,
            scalars,
            scalars,
            vectors,
            vectors,
            anywhere,
        ],
        out_specs=vectors,
        scratch_shapes=[
            pltpu.VMEM((NT + 2,) + tall, jnp.float32),
            pltpu.VMEM((NT,) + tall, jnp.float32),
            pltpu.VMEM((planes + 2 * RAD, span_y, span_z), jnp.float32),
            pltpu.VMEM((planes + 2 * RAD, span_y, span_z), jnp.float32),
            pltpu.VMEM((3, 2 * NT, span_z), jnp.float32),
            pltpu.VMEM((rows, span_z), jnp.float32),
            pltpu.VMEM((NT + 1, rows, span_z), jnp.float32),
            pltpu.VMEM((NT // 2 - 1, 2, RAD, span_y, span_z), jnp.float32),
            pltpu.VMEM((NT // 2 - 1, 2, RAD, span_y, span_z), jnp.float32),
            pltpu.VMEM((planes, span_y, span_z), jnp.float32),
            pltpu.VMEM((rows, receivers), jnp.bfloat16),
            pltpu.VMEM((receivers, span_z), jnp.float32),
            pltpu.VMEM((receivers, span_z), jnp.float32),
            pltpu.VMEM((count, span_z), jnp.float32),
            pltpu.VMEM((count, 1, span_z), jnp.float32),
            pltpu.VMEM((count, 1, span_z), jnp.float32),
            pltpu.VMEM((periods, slab, span_y, span_z), jnp.float32),
            dma((7,)),
            dma((2, NT)),
            dma((2, NT)),
            dma((2, 2)),
            dma((2, 2)),
            dma((2, NT // 2 - 1)),
            dma((2, NT // 2 - 1)),
            dma((count,)),
            dma((count,)),
            dma((periods,)),
            dma((periods,)),
        ],
        compiler_params=pltpu.CompilerParams(
            collective_id=0, has_side_effects=True, vmem_limit_bytes=63 * 1024 * 1024
        ),
    )(
        courant_sq,
        wave_now,
        wave_before,
        wavelet,
        source_cell,
        receiver_cell.reshape(1, receivers),
        send_order.reshape(1, receivers),
        observed,
    )


def solution(mesh):
    return jax.shard_map(
        per_device,
        mesh=mesh,
        in_specs=(
            P("groups", None, None),
            P(("groups", "shot"), None, None),
            P(("groups", "shot"), None, None),
            P(("groups", "shot"), None),
            P(("groups", "shot")),
            P(("groups", "shot")),
            P(("groups", "shot")),
            P(("groups", "shot"), None),
        ),
        out_specs=P(("groups", "shot"), None, None),
        check_vma=False,
    )
```

```python
import functools

import jax
import jax.numpy as jnp
from jax import lax
from jax.experimental import pallas as pl
from jax.experimental.pallas import tpu as pltpu
from jax.sharding import PartitionSpec as P

NT = 8
PIECES = 4
MESH = pl.DeviceIdType.MESH
PAD = 8

stencil_center = -205.0 / 72.0
stencil_weights = (8.0 / 5.0, -1.0 / 5.0, 8.0 / 315.0, -1.0 / 560.0)
RAD = len(stencil_weights)
DEEP = 2 * RAD


def kernel(
    count,
    courant_ref,
    now_ref,
    before_ref,
    wavelet_ref,
    source_ref,
    receiver_ref,
    order_ref,
    observed_ref,
    out_ref,
    waves,
    adjoints,
    model,
    source_mask,
    source_note,
    hits,
    scattered,
    edge_out,
    edge_in,
    image,
    row_table,
    col_table,
    spread,
    observed,
    trace_out,
    trace_in,
    parts,
    load_sem,
    halo_send,
    halo_recv,
    first_send,
    first_recv,
    edge_send,
    edge_recv,
    trace_send,
    trace_recv,
    part_send,
    part_recv,
):
    planes, span_y, span_z = now_ref.shape
    receivers = receiver_ref.shape[1]
    per_owner = receivers // count
    periods = count // PIECES
    slab = planes // periods
    rows = planes * span_y
    model_planes = courant_ref.shape[0]
    group = lax.axis_index("groups")
    me = lax.axis_index("shot")
    left = lax.rem(me + count - 1, count)
    right = lax.rem(me + 1, count)
    piece = lax.rem(me, PIECES)
    period = me // PIECES
    inner = pl.ds(PAD, span_y)
    own = pl.ds(DEEP, planes)
    half = planes // 2

    barrier = pltpu.get_barrier_semaphore()

    def greet(step, carry):
        pl.semaphore_signal(
            barrier, inc=1, device_id=(group, lax.rem(me + step, count)), device_id_type=MESH
        )
        return carry

    lax.fori_loop(1, count, greet, 0)

    trace_load = pltpu.make_async_copy(observed_ref, observed, load_sem.at[6])
    trace_load.start()
    start_plane = piece * planes
    loads = [
        pltpu.make_async_copy(now_ref, waves.at[1, own, inner], load_sem.at[0]),
        pltpu.make_async_copy(before_ref, waves.at[0, own, inner], load_sem.at[1]),
        pltpu.make_async_copy(
            courant_ref.at[pl.ds(start_plane, planes)], model.at[pl.ds(RAD, planes)], load_sem.at[2]
        ),
        pltpu.make_async_copy(
            courant_ref.at[pl.ds(lax.rem(start_plane + model_planes - RAD, model_planes), RAD)],
            model.at[pl.ds(0, RAD)],
            load_sem.at[3],
        ),
        pltpu.make_async_copy(
            courant_ref.at[pl.ds(lax.rem(start_plane + planes, model_planes), RAD)],
            model.at[pl.ds(RAD + planes, RAD)],
            load_sem.at[4],
        ),
    ]
    for load in loads:
        load.start()

    for step in range(NT):
        source_note[1, step : step + 1, :] = jnp.full((1, span_z), wavelet_ref[0, step], jnp.float32)
    cell_value = source_ref[0].astype(jnp.float32)
    source_note[1, NT : 2 * NT, :] = jnp.full((NT, span_z), cell_value, jnp.float32)

    trace_load.wait()
    for d in range(count):
        trace_out[d] = observed[d : d + 1, :]

    def neighbour(side):
        return (group, lax.rem(me + count - 1 + 2 * side, count))

    def remote(source, target, send, recv, side):
        return pltpu.make_async_remote_copy(
            src_ref=source,
            dst_ref=target,
            send_sem=send,
            recv_sem=recv,
            device_id=neighbour(side),
            device_id_type=MESH,
        )

    def halo(field, slot, exchange, side, part, source=None):
        if source is None:
            source = field.at[slot, pl.ds(DEEP + half * side + part, RAD), inner]
        return remote(
            source,
            field.at[slot, pl.ds((DEEP + planes) * (1 - side) + part, RAD), inner],
            halo_send.at[part // RAD, side, exchange],
            halo_recv.at[part // RAD, side, exchange],
            side,
        )

    def last_halo(side):
        return remote(
            adjoints.at[NT - 1, pl.ds(DEEP + (planes - RAD) * side, RAD), inner],
            adjoints.at[NT - 1, pl.ds(DEEP + planes - (planes + RAD) * side, RAD), inner],
            halo_send.at[0, side, NT - 1],
            halo_recv.at[0, side, NT - 1],
            side,
        )

    def first_halo(side, part):
        return halo(waves, 1, 0, side, part, now_ref.at[pl.ds(half * side + part, RAD)])

    def before_halo(side):
        return remote(
            before_ref.at[pl.ds((planes - RAD) * side, RAD)],
            waves.at[0, pl.ds(DEEP + planes - (planes + RAD) * side, RAD), inner],
            first_send.at[side, 0],
            first_recv.at[side, 0],
            side,
        )

    def note_copy(side):
        return remote(
            source_note.at[1],
            source_note.at[2 - 2 * side],
            first_send.at[side, 1],
            first_recv.at[side, 1],
            side,
        )

    def edge_copy(which, side):
        return remote(
            edge_out.at[which, side],
            edge_in.at[which, 1 - side],
            edge_send.at[side, which],
            edge_recv.at[side, which],
            side,
        )

    def trace_copy(step):
        peer = lax.rem(me + step, count)
        return pltpu.make_async_remote_copy(
            src_ref=trace_out.at[peer],
            dst_ref=trace_in.at[me],
            send_sem=trace_send.at[step],
            recv_sem=trace_recv.at[step],
            device_id=(group, peer),
            device_id_type=MESH,
        )

    pl.semaphore_wait(barrier, count - 1)
    for side in range(2):
        for part in range(0, DEEP, RAD):
            first_halo(side, part).start()
    for side in range(2):
        before_halo(side).start()
        note_copy(side).start()

    def trace_start(step, carry):
        trace_copy(step).start()
        return carry

    lax.fori_loop(1, count, trace_start, 0)
    own_trace = pltpu.make_async_copy(trace_out.at[me], trace_in.at[me], load_sem.at[5])
    own_trace.start()

    wide = pl.ds(DEEP - RAD, planes + 2 * RAD)
    blank = jnp.zeros((planes + 2 * RAD, PAD, span_z), jnp.float32)

    def clear(slot, carry):
        waves[slot, wide, pl.ds(0, PAD), :] = blank
        waves[slot, wide, pl.ds(PAD + span_y, PAD), :] = blank
        adjoints[slot, wide, pl.ds(0, PAD), :] = blank
        adjoints[slot, wide, pl.ds(PAD + span_y, PAD), :] = blank
        return carry

    lax.fori_loop(0, NT, clear, 0)
    waves[NT, wide, pl.ds(0, PAD), :] = blank
    waves[NT, wide, pl.ds(PAD + span_y, PAD), :] = blank
    adjoints[0, wide, inner, :] = jnp.zeros((planes + 2 * RAD, span_y, span_z), jnp.float32)

    def cells_from(plane, size):
        shape = (size * span_y, span_z)
        flat = lax.broadcasted_iota(jnp.int32, shape, 0) * span_z
        flat = flat + lax.broadcasted_iota(jnp.int32, shape, 1) + plane * (span_y * span_z)
        return flat.astype(jnp.float32)

    def mark_source(place, size, plane, owner):
        marked = jnp.where(
            cells_from(plane, size) == source_note[owner, NT : NT + 1, :], 1.0, 0.0
        )
        source_mask[pl.ds(place, size)] = marked.reshape(size, span_y, span_z)

    mark_source(RAD, planes, 0, 1)

    cells = receiver_ref[...]
    order = order_ref[...]
    down = lax.broadcasted_iota(jnp.int32, (receivers, receivers), 0)
    across = lax.broadcasted_iota(jnp.int32, (receivers, receivers), 1)
    same = down == across
    cells_col = jnp.sum(jnp.where(same, cells, 0), axis=1, keepdims=True)
    order_col = jnp.sum(jnp.where(same, order, 0), axis=1, keepdims=True)
    owned_row = jnp.sum(jnp.where(down == order, cells_col, 0), axis=0, keepdims=True)
    owned_col = jnp.sum(jnp.where(across == order_col, cells, 0), axis=1, keepdims=True)
    row_table[...] = jnp.where(
        owned_row // span_z == lax.broadcasted_iota(jnp.int32, (rows, receivers), 0), 1.0, 0.0
    ).astype(jnp.bfloat16)
    col_hot = jnp.where(
        lax.rem(owned_col, span_z) == lax.broadcasted_iota(jnp.int32, (receivers, span_z), 1),
        1.0,
        0.0,
    )
    col_table[...] = col_hot
    hits[...] = jnp.dot(
        row_table[...], col_hot.astype(jnp.bfloat16), preferred_element_type=jnp.float32
    )

    lane = lax.broadcasted_iota(jnp.int32, (1, 1, span_z), 2)
    lane_weights = []
    for distance in range(1, RAD + 1):
        weight = stencil_weights[distance - 1]
        lane_weights.append(
            (
                jnp.where(lane >= distance, weight, 0.0),
                jnp.where(lane < span_z - distance, weight, 0.0),
            )
        )

    def advanced(field, now, start, size=RAD):
        tiles = []
        for row in range(0, span_y, PAD):
            column = field[
                now, pl.ds(start + DEEP - RAD, size + 2 * RAD), pl.ds(PAD + row, PAD), :
            ]
            here = pl.ds(start + DEEP, size)
            center = column[RAD : RAD + size]
            total = (3.0 * stencil_center) * center
            for distance in range(1, RAD + 1):
                beside = (
                    column[RAD + distance : RAD + distance + size]
                    + column[RAD - distance : RAD - distance + size]
                )
                beside = beside + (
                    field[now, here, pl.ds(PAD + row + distance, PAD), :]
                    + field[now, here, pl.ds(PAD + row - distance, PAD), :]
                )
                up, low = lane_weights[distance - 1]
                total = total + stencil_weights[distance - 1] * beside
                total = total + (
                    up * pltpu.roll(center, distance, 2)
                    + low * pltpu.roll(center, span_z - distance, 2)
                )
            tiles.append(
                2.0 * center
                - field[now - 1, here, pl.ds(PAD + row, PAD), :]
                + model[pl.ds(start + RAD, size), pl.ds(row, PAD), :] * total
            )
        return jnp.concatenate(tiles, axis=1)

    def plane_rows(plane):
        return pl.ds(pl.multiple_of(plane * span_y, span_y), span_y)

    def store(field, slot, start, made):
        for i in range(len(made)):
            field[slot, start + i + DEEP, inner, :] = made[i]

    def forward_planes(step, start, owner=1):
        amount = source_note[owner, pl.ds(step, 1), :]
        ahead = advanced(waves, step + 1, start)
        made = [ahead[i] + amount * source_mask[start + i + RAD] for i in range(RAD)]
        store(waves, step + 2, start, made)
        return made

    def sources(step, plane, wave):
        return hits[plane_rows(plane), :] * wave - scattered[step, plane_rows(plane), :]

    def adjoint_planes(step, start, size=RAD):
        made = []
        ahead = advanced(adjoints, step, start, size)
        for i in range(size):
            plane = start + i
            wave = waves[NT + 1 - step, plane + DEEP, inner, :]
            made.append(ahead[i] + sources(NT - 1 - step, plane, wave))
        return made

    def adjoint_keep(step, start):
        store(adjoints, step + 1, start, adjoint_planes(step, start))

    def adjoint_beside(step, start, which, side):
        ahead = advanced(adjoints, step, start)
        made = [ahead[i] + edge_in[which, side, i] for i in range(RAD)]
        store(adjoints, step + 1, start, made)

    def send_edges(which, step, side):
        start = (planes - RAD) * side
        for i in range(RAD):
            wave = waves[step + 2, start + i + DEEP, inner, :]
            edge_out[which, side, i] = sources(step, start + i, wave)
        edge_copy(which, side).start()

    middle = range(RAD, planes - RAD, RAD)

    def spread_traces():
        own_trace.wait()

        def arrived(step, carry):
            trace_copy(step).wait_recv()
            return carry

        lax.fori_loop(1, count, arrived, 0)
        repeated = jnp.broadcast_to(trace_in[...], (count, per_owner, span_z)).reshape(
            receivers, span_z
        )
        slot_of = lax.rem(lax.broadcasted_iota(jnp.int32, (receivers, span_z), 0), per_owner)
        lane_slot = lax.rem(lax.broadcasted_iota(jnp.int32, (receivers, span_z), 1), per_owner)
        spread[...] = jnp.where(slot_of == lane_slot, repeated, 0.0)

    lane_step = lax.broadcasted_iota(jnp.int32, (span_z, span_z), 0) // per_owner

    def scatter(step):
        chosen = jnp.where(lane_step == step, 1.0, 0.0)
        values = jnp.dot(
            spread[...],
            chosen,
            precision=lax.Precision.HIGHEST,
            preferred_element_type=jnp.float32,
        )
        weighted = col_table[...] * values
        total = None
        for _ in range(3):
            piece_of = weighted.astype(jnp.bfloat16)
            weighted = weighted - piece_of.astype(jnp.float32)
            term = jnp.dot(row_table[...], piece_of, preferred_element_type=jnp.float32)
            total = term if total is None else total + term
        scattered[step] = total

    for load in loads:
        load.wait()

    first_side = lax.rem(me, 2)

    def forward_pair(pair, begin_adjoint):
        step = 2 * pair
        for start in middle:
            forward_planes(step, start)

        def one_side(turn, carry):
            side = lax.rem(first_side + turn, 2)
            for part in range(0, DEEP, RAD):
                halo(waves, step + 1, pair, 1 - side, part).wait_recv()

            if not begin_adjoint:

                @pl.when(pair == 0)
                def _():
                    before_halo(1 - side).wait_recv()
                    note_copy(1 - side).wait_recv()
                    mark_source(
                        (planes + RAD) * side, RAD, (planes - RAD) * (1 - side), 2 * side
                    )

            forward_planes(step, (planes + RAD) * side - RAD, 2 * side)
            forward_planes(step, (planes - RAD) * side)
            for part in range(0, half, RAD):
                start = half * side + part
                made = forward_planes(step + 1, start)
                if begin_adjoint:
                    first = [
                        sources(NT - 1, start + i, made[i]) for i in range(RAD)
                    ]
                    store(adjoints, 1, start, first)
                    halo(adjoints, 1, NT // 2, side, part).start()
                else:
                    halo(waves, step + 3, pair + 1, side, part).start()
            if begin_adjoint:
                send_edges(NT // 2 - 2, NT - 2, side)
            return carry

        lax.fori_loop(0, 2, one_side, 0)

    def forward_loop(pair, carry):
        forward_pair(pair, False)

        @pl.when(pair == 0)
        def _():
            spread_traces()

        for i in range(3):
            scatter(3 * pair + i)

        @pl.when(pair > 0)
        def _():
            for side in range(2):
                send_edges(pair - 1, 2 * pair, side)

        return carry

    lax.fori_loop(0, NT // 2 - 1, forward_loop, 0)
    forward_pair(NT // 2 - 1, True)

    def add_image(step):
        for plane in range(planes):
            image[plane] += (
                adjoints[step, plane + DEEP, inner, :]
                * waves[NT + 2 - step, plane + DEEP, inner, :]
            )

    image[...] = jnp.zeros((planes, span_y, span_z), jnp.float32)

    def adjoint_pair(pair, last):
        step = 2 * pair + 1
        which = NT // 2 - 2 - pair
        for start in middle:
            adjoint_keep(step, start)

        def one_side(turn, carry):
            side = lax.rem(first_side + turn, 2)
            for part in range(0, DEEP, RAD):
                halo(adjoints, step, NT // 2 + pair, 1 - side, part).wait_recv()
            edge_copy(which, 1 - side).wait_recv()
            adjoint_beside(step, (planes + RAD) * side - RAD, which, side)
            adjoint_keep(step, (planes - RAD) * side)
            if last:
                adjoint_keep(step + 1, (planes - RAD) * side)
                last_halo(side).start()
            else:
                for part in range(0, half, RAD):
                    adjoint_keep(step + 1, half * side + part)
                    halo(adjoints, step + 2, NT // 2 + pair + 1, side, part).start()
            return carry

        lax.fori_loop(0, 2, one_side, 0)
        if last:
            for start in middle:
                adjoint_keep(step + 1, start)
        add_image(step)
        add_image(step + 1)

    def adjoint_loop(pair, carry):
        adjoint_pair(pair, False)
        return carry

    lax.fori_loop(0, NT // 2 - 2, adjoint_loop, 0)
    adjoint_pair(NT // 2 - 2, True)
    add_image(NT - 1)

    def part_copy(step):
        target = lax.rem(period + step, periods)
        return pltpu.make_async_remote_copy(
            src_ref=image.at[pl.ds(target * slab, slab)],
            dst_ref=parts.at[step],
            send_sem=part_send.at[step],
            recv_sem=part_recv.at[step],
            device_id=(group, target * PIECES + piece),
            device_id_type=MESH,
        )

    def finish(start):
        made = adjoint_planes(NT - 1, start, slab)
        return [
            image[start + i] + made[i] * waves[2, start + i + DEEP, inner, :] for i in range(slab)
        ]

    def send_part(which, carry):
        start = which * slab
        made = finish(start)
        for i in range(slab):
            image[start + i] = made[i]

        @pl.when(which != period)
        def _():
            part_copy(lax.rem(which - period + periods, periods)).start()

        return carry

    low, high = RAD // slab, (planes - RAD) // slab
    lax.fori_loop(low, high, send_part, 0)
    for side in range(2):
        last_halo(side).wait_recv()
    lax.fori_loop(0, low, send_part, 0)
    lax.fori_loop(high, periods, send_part, 0)
    for i in range(slab):
        out_ref[i] = image[period * slab + i]

    for side in range(2):
        for part in range(0, DEEP, RAD):
            first_halo(side, part).wait_send()
        before_halo(side).wait_send()
        note_copy(side).wait_send()
        last_halo(side).wait_send()
        for pair in range(1, NT // 2):
            for part in range(0, DEEP, RAD):
                halo(waves, 2 * pair + 1, pair, side, part).wait_send()
                halo(adjoints, 2 * pair - 1, NT // 2 + pair - 1, side, part).wait_send()
            edge_copy(pair - 1, side).wait_send()

    def sent_trace(step, carry):
        trace_copy(step).wait_send()
        return carry

    lax.fori_loop(1, count, sent_trace, 0)

    def add_part(step, carry):
        part_copy(step).wait_recv()
        out_ref[...] += parts[step]
        return carry

    lax.fori_loop(1, periods, add_part, 0)

    def sent_part(step, carry):
        part_copy(step).wait_send()
        return carry

    lax.fori_loop(1, periods, sent_part, 0)


def per_device(
    courant_sq, wave_now, wave_before, wavelet, source_cell, receiver_cell, send_order, observed
):
    count = lax.axis_size("shot")
    planes, span_y, span_z = wave_now.shape
    receivers = receiver_cell.shape[0]
    periods = count // PIECES
    slab = planes // periods
    rows = planes * span_y
    tall = (planes + 2 * DEEP, span_y + 2 * PAD, span_z)
    anywhere = pl.BlockSpec(memory_space=pltpu.HBM)
    scalars = pl.BlockSpec(memory_space=pltpu.SMEM)
    vectors = pl.BlockSpec(memory_space=pltpu.VMEM)
    dma = pltpu.SemaphoreType.DMA
    return pl.pallas_call(
        functools.partial(kernel, count),
        out_shape=jax.ShapeDtypeStruct((slab, span_y, span_z), jnp.float32),
        in_specs=[
            anywhere,
            anywhere,
            anywhere,
            scalars,
            scalars,
            vectors,
            vectors,
            anywhere,
        ],
        out_specs=vectors,
        scratch_shapes=[
            pltpu.VMEM((NT + 2,) + tall, jnp.float32),
            pltpu.VMEM((NT,) + tall, jnp.float32),
            pltpu.VMEM((planes + 2 * RAD, span_y, span_z), jnp.float32),
            pltpu.VMEM((planes + 2 * RAD, span_y, span_z), jnp.float32),
            pltpu.VMEM((3, 2 * NT, span_z), jnp.float32),
            pltpu.VMEM((rows, span_z), jnp.float32),
            pltpu.VMEM((NT + 1, rows, span_z), jnp.float32),
            pltpu.VMEM((NT // 2 - 1, 2, RAD, span_y, span_z), jnp.float32),
            pltpu.VMEM((NT // 2 - 1, 2, RAD, span_y, span_z), jnp.float32),
            pltpu.VMEM((planes, span_y, span_z), jnp.float32),
            pltpu.VMEM((rows, receivers), jnp.bfloat16),
            pltpu.VMEM((receivers, span_z), jnp.float32),
            pltpu.VMEM((receivers, span_z), jnp.float32),
            pltpu.VMEM((count, span_z), jnp.float32),
            pltpu.VMEM((count, 1, span_z), jnp.float32),
            pltpu.VMEM((count, 1, span_z), jnp.float32),
            pltpu.VMEM((periods, slab, span_y, span_z), jnp.float32),
            dma((7,)),
            dma((2, 2, NT)),
            dma((2, 2, NT)),
            dma((2, 2)),
            dma((2, 2)),
            dma((2, NT // 2 - 1)),
            dma((2, NT // 2 - 1)),
            dma((count,)),
            dma((count,)),
            dma((periods,)),
            dma((periods,)),
        ],
        compiler_params=pltpu.CompilerParams(
            collective_id=0, has_side_effects=True, vmem_limit_bytes=63 * 1024 * 1024
        ),
    )(
        courant_sq,
        wave_now,
        wave_before,
        wavelet,
        source_cell,
        receiver_cell.reshape(1, receivers),
        send_order.reshape(1, receivers),
        observed,
    )


def solution(mesh):
    return jax.shard_map(
        per_device,
        mesh=mesh,
        in_specs=(
            P("groups", None, None),
            P(("groups", "shot"), None, None),
            P(("groups", "shot"), None, None),
            P(("groups", "shot"), None),
            P(("groups", "shot")),
            P(("groups", "shot")),
            P(("groups", "shot")),
            P(("groups", "shot"), None),
        ),
        out_specs=P(("groups", "shot"), None, None),
        check_vma=False,
    )
```
